32 devices in a mesh: wide: 16 (over z, y, x), narrow: 2 (over core).
Axes of the slice: x: 2, y: 2, z: 4, core: 2. Of those that a mesh axis runs over, the one named last changes fastest.
Arguments:
- x_trial: float32 [2, 512, 512], P(None, 'wide', 'narrow'), may hold values from -6 to 6
- psi_orb: float32 [512, 16384], P('narrow', 'wide'), may hold values from -0.046875 to 0.046875
- phi_orb: float32 [512, 16384], P('wide', 'narrow'), may hold values from -0.046875 to 0.046875
- screened: float32 [16384, 16384], P('wide', 'narrow'), may hold values from -192 to 192
- eps_val: float32 [512], P('wide'), may hold values from -1 to -0.1
- eps_cond: float32 [512], P('narrow'), may hold values from 0.1 to 1
Outputs:
- applied: float32 [2, 512, 512], P(None, 'wide', 'narrow')
The draws below stay inside these ranges and needn't reach their ends.
All inputs are finite; a program needn't handle non-finite values.
Results may differ from the reference program's by a relative error of at most 0.00011.
Values sent between devices are 32-bit elements; how exact they have to be, the bound alone decides.
A program may use at most 192 MiB of HBM per device.

```python
import jax
import jax.numpy as jnp
from jax import lax

NV = 512
NC = 512
NP = 16384
NT = 2


def block_levels(stream_key, extent, shards, low, largest):
    level = 1.0
    for dim, shards_of in shards:
        draws = jax.random.uniform(jax.random.fold_in(jax.random.fold_in(stream_key, 6), dim), (shards_of,), jnp.float32, low / len(shards), largest / len(shards))
        level = level * jnp.repeat(jnp.exp(draws), extent[dim] // shards_of).reshape((-1,) + (1,) * (len(extent) - 1 - dim))
    return level


def bell_draw(stream_key, shape, spread, most, cuts=(), held_as=jnp.bfloat16):
    gain = block_levels(stream_key, shape, cuts, -0.22, 0.18) if cuts else 1.0
    values = jax.random.normal(stream_key, shape, jnp.float32) * spread * gain
    return jnp.minimum(jnp.maximum(values, -most), most).astype(held_as)


def setup_inputs(seed: int = 0) -> dict:
    streams_of = jax.random.split(jax.random.key(seed), 7)
    x_trial = bell_draw(streams_of[0], (NT, NV, NC), 1.0, 6.0, ((1, 16), (2, 2)), jnp.float32)
    psi_orb = bell_draw(streams_of[1], (NV, NP), (NP ** -0.5), 0.046875, ((0, 2), (1, 16)), jnp.float32)
    phi_orb = bell_draw(streams_of[2], (NC, NP), (NP ** -0.5), 0.046875, ((0, 16), (1, 2)), jnp.float32)
    screened = bell_draw(streams_of[3], (NP, NP), (NP / (NV * NC) ** 0.5), 192.0, ((0, 16), (1, 2)), jnp.float32)
    eps_val = jnp.clip(-1.0 + 0.9 * jax.random.uniform(streams_of[4], (NV,), jnp.float32) ** block_levels(streams_of[4], (NV,), ((0, 16),), -0.2, 0.2), -1.0, -0.1)
    eps_cond = jnp.clip(0.1 + 0.9 * jax.random.uniform(streams_of[5], (NC,), jnp.float32) ** block_levels(streams_of[5], (NC,), ((0, 2),), -0.2, 0.2), 0.1, 1.0)
    return dict(x_trial=x_trial, psi_orb=psi_orb, phi_orb=phi_orb, screened=screened, eps_val=eps_val, eps_cond=eps_cond)


def reference(x_trial, psi_orb, phi_orb, screened, eps_val, eps_cond):
    precise = lax.Precision.HIGHEST
    half_map = jnp.einsum("vr,tvc->trc", psi_orb, x_trial, precision=precise)
    block = NP // 16
    blocks = NP // block
    screen_blocks = screened.reshape(blocks, block, NP)
    half_blocks = jnp.transpose(half_map.reshape(NT, blocks, block, NC), (1, 0, 2, 3))

    def one_block(pieces):
        half_piece, screen_piece = pieces
        pair_tile = jnp.einsum("trc,cs->trs", half_piece, phi_orb, precision=precise) * screen_piece[None]
        return jnp.einsum("trs,cs->trc", pair_tile, phi_orb, precision=precise)

    back_blocks = lax.map(one_block, (half_blocks, screen_blocks))
    back_map = jnp.transpose(back_blocks, (1, 0, 2, 3)).reshape(NT, NP, NC)
    kernel = jnp.einsum("vr,trc->tvc", psi_orb, back_map, precision=precise)
    energy_gap = eps_cond[None, None, :] - eps_val[None, :, None]
    return kernel + energy_gap * x_trial
```

```python
import functools
import math

import jax
import jax.numpy as jnp
from jax import lax
from jax.experimental import pallas as pl
from jax.experimental.pallas import tpu as pltpu
from jax.sharding import PartitionSpec as P

MESH = pl.DeviceIdType.MESH
VM = pl.BlockSpec(memory_space=pltpu.VMEM)
CHUNKS = (2, 2, 2, 1, 1)


def spread_kernel(n, m, x_ref, psi_ref, xs_ref, psis_ref, xs_sem, xr_sem, fs_sem, fr_sem, ps_sem, pr_sem, own_sem):
    w = lax.axis_index("wide")
    c = lax.axis_index("narrow")

    def psi_copy(slot, peer, k):
        return pltpu.make_async_remote_copy(
            src_ref=psi_ref, dst_ref=psis_ref.at[slot], send_sem=ps_sem.at[k], recv_sem=pr_sem.at[slot],
            device_id=(w, peer), device_id_type=MESH)

    def x_copy(slot, peer, k):
        return pltpu.make_async_remote_copy(
            src_ref=x_ref, dst_ref=xs_ref.at[c, slot], send_sem=xs_sem.at[k], recv_sem=xr_sem.at[slot],
            device_id=(peer, c), device_id_type=MESH)

    def forward(src, slot_c, slot, peer, k):
        return pltpu.make_async_remote_copy(
            src_ref=src, dst_ref=xs_ref.at[slot_c, slot], send_sem=fs_sem.at[k, slot],
            recv_sem=fr_sem.at[slot_c, slot], device_id=(w, peer), device_id_type=MESH)

    @pl.loop(1, n)
    def _(i):
        x_copy(w, lax.rem(w + i, n), i).start()

    @pl.loop(1, m)
    def _(j):
        forward(x_ref, c, w, lax.rem(c + j, m), j).start()
        psi_copy(c, lax.rem(c + j, m), j).start()

    own_x = pltpu.make_async_copy(x_ref, xs_ref.at[c, w], own_sem.at[0])
    own_psi = pltpu.make_async_copy(psi_ref, psis_ref.at[c], own_sem.at[1])
    own_x.start()
    own_psi.start()

    @pl.loop(1, n)
    def _(i):
        src = lax.rem(w + n - i, n)
        x_copy(src, w, i).wait_recv()

        @pl.loop(1, m)
        def _(j):
            forward(xs_ref.at[c, src], c, src, lax.rem(c + j, m), j).start()

    own_x.wait()
    own_psi.wait()

    @pl.loop(1, m)
    def _(j):
        other = lax.rem(c + m - j, m)
        psi_copy(other, c, j).wait_recv()
        psi_copy(c, c, j).wait_send()

        @pl.loop(0, n)
        def _(i):
            forward(x_ref, other, i, c, j).wait_recv()
            forward(x_ref, c, i, c, j).wait_send()

    @pl.loop(1, n)
    def _(i):
        x_copy(w, w, i).wait_send()


def spread(n, m, x_trial, psi_orb):
    return pl.pallas_call(
        functools.partial(spread_kernel, n, m),
        out_shape=(
            jax.ShapeDtypeStruct((m, n) + x_trial.shape, jnp.float32),
            jax.ShapeDtypeStruct((m,) + psi_orb.shape, jnp.float32),
        ),
        in_specs=[VM, VM],
        out_specs=(VM, VM),
        scratch_shapes=[
            pltpu.SemaphoreType.DMA((n,)),
            pltpu.SemaphoreType.DMA((n,)),
            pltpu.SemaphoreType.DMA((m, n)),
            pltpu.SemaphoreType.DMA((m, n)),
            pltpu.SemaphoreType.DMA((m,)),
            pltpu.SemaphoreType.DMA((m,)),
            pltpu.SemaphoreType.DMA((2,)),
        ],
        compiler_params=pltpu.CompilerParams(has_side_effects=True),
        name="spread",
    )(x_trial, psi_orb)


def collect_kernel(n, part_ref, out_ref, got, s_sem, r_sem):
    w = lax.axis_index("wide")
    c = lax.axis_index("narrow")

    def copy(block, slot, peer, k):
        return pltpu.make_async_remote_copy(
            src_ref=part_ref.at[block], dst_ref=got.at[slot], send_sem=s_sem.at[k], recv_sem=r_sem.at[slot],
            device_id=(peer, c), device_id_type=MESH)

    @pl.loop(1, n)
    def _(i):
        peer = lax.rem(w + i, n)
        copy(peer, w, peer, i).start()

    out_ref[...] = part_ref[w]

    @pl.loop(1, n)
    def _(i):
        src = lax.rem(w + n - i, n)
        copy(src, src, w, i).wait_recv()
        out_ref[...] += got[src]

    @pl.loop(1, n)
    def _(i):
        copy(w, w, w, i).wait_send()


def collect(n, part):
    return pl.pallas_call(
        functools.partial(collect_kernel, n),
        out_shape=jax.ShapeDtypeStruct(part.shape[1:], jnp.float32),
        in_specs=[VM],
        out_specs=VM,
        scratch_shapes=[
            pltpu.VMEM(part.shape, jnp.float32),
            pltpu.SemaphoreType.DMA((n,)),
            pltpu.SemaphoreType.DMA((n,)),
        ],
        compiler_params=pltpu.CompilerParams(has_side_effects=True),
        name="collect",
    )(part)


def halves(a):
    high = a.astype(jnp.bfloat16)
    return high, (a - high.astype(jnp.float32)).astype(jnp.bfloat16)


def dot3(a, b, dims):
    def one(p, q):
        return lax.dot_general(p, q, (dims, ((), ())), preferred_element_type=jnp.float32)

    return one(a[0], b[0]) + (one(a[0], b[1]) + one(a[1], b[0]))


def tile_kernel(first, rows, half_ref, phi_ref, screened_ref, *refs):
    if first:
        back_ref, high, low = refs
    else:
        sum_ref, back_ref, high, low = refs
    trials, points, _ = half_ref.shape
    steps = points // rows

    @pl.when(pl.program_id(0) == 0)
    def _():
        for t in range(trials):
            @pl.loop(0, steps)
            def _(r):
                at = pl.ds(pl.multiple_of(r * rows, rows), rows)
                high[t, at], low[t, at] = halves(half_ref[t, at])
                back_ref[t, at] = jnp.zeros_like(half_ref[t, at]) if first else sum_ref[t, at]

    phi = halves(phi_ref[...])

    @pl.loop(0, steps)
    def _(r):
        at = pl.ds(pl.multiple_of(r * rows, rows), rows)
        for t in range(trials):
            pair = dot3((high[t, at], low[t, at]), phi, ((1,), (0,))) * screened_ref[at]
            back_ref[t, at] += dot3(halves(pair), phi, ((1,), (1,)))


def tile(half_map, phi, screened, start, back):
    trials, points, orbitals = half_map.shape
    width = phi.shape[1]
    columns = math.gcd(math.gcd(width, start) if start else width, 512)
    rows = math.gcd(points, 256)
    offset = start // columns
    whole = pl.BlockSpec((trials, points, orbitals), lambda s: (0, 0, 0))
    specs = [
        whole,
        pl.BlockSpec((orbitals, columns), lambda s: (0, s)),
        pl.BlockSpec((points, columns), lambda s: (0, s + offset)),
    ]
    args = [half_map, phi, screened]
    if back is not None:
        specs.append(whole)
        args.append(back)
    return pl.pallas_call(
        functools.partial(tile_kernel, back is None, rows),
        grid=(width // columns,),
        out_shape=jax.ShapeDtypeStruct(half_map.shape, jnp.float32),
        in_specs=specs,
        out_specs=whole,
        scratch_shapes=[pltpu.VMEM(half_map.shape, jnp.bfloat16)] * 2,
        input_output_aliases={3: 0} if back is not None else {},
        cost_estimate=pl.CostEstimate(
            flops=12 * trials * points * orbitals * width,
            bytes_accessed=4 * (points * width + orbitals * width + 3 * trials * points * orbitals),
            transcendentals=0,
        ),
        name="tile",
    )(*args)


def local(n, m, x_trial, psi_orb, phi_orb, screened, eps_val, eps_cond):
    high = lax.Precision.HIGH
    width = phi_orb.shape[1]
    unit = width // sum(CHUNKS)
    phi_cols, start = [], 0
    for count in CHUNKS:
        piece = lax.slice_in_dim(phi_orb, start, start + count * unit, axis=1)
        phi_cols.append((start, lax.all_gather(piece, "wide", axis=0, tiled=True)))
        start += count * unit
    x_all, psi_all = spread(n, m, x_trial, psi_orb)
    trials, vals, conds = x_trial.shape
    psi_rows = psi_all.reshape(m * psi_orb.shape[0], psi_orb.shape[1])
    x_whole = jnp.transpose(x_all, (2, 1, 3, 0, 4)).reshape(trials, n * vals, m * conds)
    back = None
    half_map = jnp.einsum("vr,tvc->trc", psi_rows, x_whole, precision=high)
    for start, phi in phi_cols:
        back = tile(half_map, phi, screened, start, back)
    summed = lax.psum_scatter(back, "narrow", scatter_dimension=2, tiled=True)
    part = jnp.einsum("vr,trc->vtc", psi_rows, summed, precision=high)
    part = jnp.swapaxes(part.reshape(n, vals, trials, conds), 1, 2)
    kernel = collect(n, part)
    energy_gap = eps_cond[None, None, :] - eps_val[None, :, None]
    return kernel + energy_gap * x_trial


def solution(mesh):
    placed = (
        P(None, "wide", "narrow"),
        P("narrow", "wide"),
        P("wide", "narrow"),
        P("wide", "narrow"),
        P("wide"),
        P("narrow"),
    )
    return jax.shard_map(
        functools.partial(local, mesh.shape["wide"], mesh.shape["narrow"]),
        mesh=mesh, in_specs=placed, out_specs=P(None, "wide", "narrow"), check_vma=False,
    )
```

```python
import functools
import math

import jax
import jax.numpy as jnp
from jax import lax
from jax.experimental import pallas as pl
from jax.experimental.pallas import tpu as pltpu
from jax.sharding import PartitionSpec as P

MESH = pl.DeviceIdType.MESH
VM = pl.BlockSpec(memory_space=pltpu.VMEM)
CHUNKS = (5, 3)


def spread_kernel(n, m, x_ref, psi_ref, xs_ref, psis_ref, xs_sem, xr_sem, fs_sem, fr_sem, ps_sem, pr_sem, own_sem):
    w = lax.axis_index("wide")
    c = lax.axis_index("narrow")

    def psi_copy(slot, peer, k):
        return pltpu.make_async_remote_copy(
            src_ref=psi_ref, dst_ref=psis_ref.at[slot], send_sem=ps_sem.at[k], recv_sem=pr_sem.at[slot],
            device_id=(w, peer), device_id_type=MESH)

    def x_copy(slot, peer, k):
        return pltpu.make_async_remote_copy(
            src_ref=x_ref, dst_ref=xs_ref.at[c, slot], send_sem=xs_sem.at[k], recv_sem=xr_sem.at[slot],
            device_id=(peer, c), device_id_type=MESH)

    def forward(src, slot_c, slot, peer, k):
        return pltpu.make_async_remote_copy(
            src_ref=src, dst_ref=xs_ref.at[slot_c, slot], send_sem=fs_sem.at[k, slot],
            recv_sem=fr_sem.at[slot_c, slot], device_id=(w, peer), device_id_type=MESH)

    @pl.loop(1, n)
    def _(i):
        x_copy(w, lax.rem(w + i, n), i).start()

    @pl.loop(1, m)
    def _(j):
        forward(x_ref, c, w, lax.rem(c + j, m), j).start()
        psi_copy(c, lax.rem(c + j, m), j).start()

    own_x = pltpu.make_async_copy(x_ref, xs_ref.at[c, w], own_sem.at[0])
    own_psi = pltpu.make_async_copy(psi_ref, psis_ref.at[c], own_sem.at[1])
    own_x.start()
    own_psi.start()

    @pl.loop(1, n)
    def _(i):
        src = lax.rem(w + n - i, n)
        x_copy(src, w, i).wait_recv()

        @pl.loop(1, m)
        def _(j):
            forward(xs_ref.at[c, src], c, src, lax.rem(c + j, m), j).start()

    own_x.wait()
    own_psi.wait()

    @pl.loop(1, m)
    def _(j):
        other = lax.rem(c + m - j, m)
        psi_copy(other, c, j).wait_recv()
        psi_copy(c, c, j).wait_send()

        @pl.loop(0, n)
        def _(i):
            forward(x_ref, other, i, c, j).wait_recv()
            forward(x_ref, c, i, c, j).wait_send()

    @pl.loop(1, n)
    def _(i):
        x_copy(w, w, i).wait_send()


def spread(n, m, x_trial, psi_orb):
    return pl.pallas_call(
        functools.partial(spread_kernel, n, m),
        out_shape=(
            jax.ShapeDtypeStruct((m, n) + x_trial.shape, jnp.float32),
            jax.ShapeDtypeStruct((m,) + psi_orb.shape, jnp.float32),
        ),
        in_specs=[VM, VM],
        out_specs=(VM, VM),
        scratch_shapes=[
            pltpu.SemaphoreType.DMA((n,)),
            pltpu.SemaphoreType.DMA((n,)),
            pltpu.SemaphoreType.DMA((m, n)),
            pltpu.SemaphoreType.DMA((m, n)),
            pltpu.SemaphoreType.DMA((m,)),
            pltpu.SemaphoreType.DMA((m,)),
            pltpu.SemaphoreType.DMA((2,)),
        ],
        compiler_params=pltpu.CompilerParams(has_side_effects=True),
        name="spread",
    )(x_trial, psi_orb)


def collect_kernel(n, part_ref, out_ref, got, s_sem, r_sem):
    w = lax.axis_index("wide")
    c = lax.axis_index("narrow")

    def copy(block, slot, peer, k):
        return pltpu.make_async_remote_copy(
            src_ref=part_ref.at[block], dst_ref=got.at[slot], send_sem=s_sem.at[k], recv_sem=r_sem.at[slot],
            device_id=(peer, c), device_id_type=MESH)

    @pl.loop(1, n)
    def _(i):
        peer = lax.rem(w + i, n)
        copy(peer, w, peer, i).start()

    out_ref[...] = part_ref[w]

    @pl.loop(1, n)
    def _(i):
        src = lax.rem(w + n - i, n)
        copy(src, src, w, i).wait_recv()
        out_ref[...] += got[src]

    @pl.loop(1, n)
    def _(i):
        copy(w, w, w, i).wait_send()


def collect(n, part):
    return pl.pallas_call(
        functools.partial(collect_kernel, n),
        out_shape=jax.ShapeDtypeStruct(part.shape[1:], jnp.float32),
        in_specs=[VM],
        out_specs=VM,
        scratch_shapes=[
            pltpu.VMEM(part.shape, jnp.float32),
            pltpu.SemaphoreType.DMA((n,)),
            pltpu.SemaphoreType.DMA((n,)),
        ],
        compiler_params=pltpu.CompilerParams(has_side_effects=True),
        name="collect",
    )(part)


def halves(a):
    high = a.astype(jnp.bfloat16)
    return high, (a - high.astype(jnp.float32)).astype(jnp.bfloat16)


def dot3(a, b, dims):
    def one(p, q):
        return lax.dot_general(p, q, (dims, ((), ())), preferred_element_type=jnp.float32)

    return one(a[0], b[0]) + (one(a[0], b[1]) + one(a[1], b[0]))


def tile_kernel(first, rows, half_ref, phi_ref, screened_ref, *refs):
    if first:
        back_ref, high, low = refs
    else:
        sum_ref, back_ref, high, low = refs
    trials, points, _ = half_ref.shape
    steps = points // rows

    @pl.when(pl.program_id(0) == 0)
    def _():
        for t in range(trials):
            @pl.loop(0, steps)
            def _(r):
                at = pl.ds(pl.multiple_of(r * rows, rows), rows)
                high[t, at], low[t, at] = halves(half_ref[t, at])
                back_ref[t, at] = jnp.zeros_like(half_ref[t, at]) if first else sum_ref[t, at]

    phi = halves(phi_ref[...])

    @pl.loop(0, steps)
    def _(r):
        at = pl.ds(pl.multiple_of(r * rows, rows), rows)
        for t in range(trials):
            pair = dot3((high[t, at], low[t, at]), phi, ((1,), (0,))) * screened_ref[at]
            back_ref[t, at] += dot3(halves(pair), phi, ((1,), (1,)))


def tile(half_map, phi, screened, start, back):
    trials, points, orbitals = half_map.shape
    width = phi.shape[1]
    columns = math.gcd(math.gcd(width, start) if start else width, 512)
    rows = math.gcd(points, 256)
    offset = start // columns
    whole = pl.BlockSpec((trials, points, orbitals), lambda s: (0, 0, 0))
    specs = [
        whole,
        pl.BlockSpec((orbitals, columns), lambda s: (0, s)),
        pl.BlockSpec((points, columns), lambda s: (0, s + offset)),
    ]
    args = [half_map, phi, screened]
    if back is not None:
        specs.append(whole)
        args.append(back)
    return pl.pallas_call(
        functools.partial(tile_kernel, back is None, rows),
        grid=(width // columns,),
        out_shape=jax.ShapeDtypeStruct(half_map.shape, jnp.float32),
        in_specs=specs,
        out_specs=whole,
        scratch_shapes=[pltpu.VMEM(half_map.shape, jnp.bfloat16)] * 2,
        input_output_aliases={3: 0} if back is not None else {},
        cost_estimate=pl.CostEstimate(
            flops=12 * trials * points * orbitals * width,
            bytes_accessed=4 * (points * width + orbitals * width + 3 * trials * points * orbitals),
            transcendentals=0,
        ),
        name="tile",
    )(*args)


def local(n, m, x_trial, psi_orb, phi_orb, screened, eps_val, eps_cond):
    high = lax.Precision.HIGH
    width = phi_orb.shape[1]
    unit = width // sum(CHUNKS)
    phi_cols, start = [], 0
    for count in CHUNKS:
        piece = lax.slice_in_dim(phi_orb, start, start + count * unit, axis=1)
        phi_cols.append((start, lax.all_gather(piece, "wide", axis=0, tiled=True)))
        start += count * unit
    x_all, psi_all = spread(n, m, x_trial, psi_orb)
    trials, vals, conds = x_trial.shape
    psi_rows = psi_all.reshape(m * psi_orb.shape[0], psi_orb.shape[1])
    x_whole = jnp.transpose(x_all, (2, 1, 3, 0, 4)).reshape(trials, n * vals, m * conds)
    back = None
    half_map = jnp.einsum("vr,tvc->trc", psi_rows, x_whole, precision=high)
    for start, phi in phi_cols:
        back = tile(half_map, phi, screened, start, back)
    summed = lax.psum_scatter(back, "narrow", scatter_dimension=2, tiled=True)
    part = jnp.einsum("vr,trc->vtc", psi_rows, summed, precision=high)
    part = jnp.swapaxes(part.reshape(n, vals, trials, conds), 1, 2)
    kernel = collect(n, part)
    energy_gap = eps_cond[None, None, :] - eps_val[None, :, None]
    return kernel + energy_gap * x_trial


def solution(mesh):
    placed = (
        P(None, "wide", "narrow"),
        P("narrow", "wide"),
        P("wide", "narrow"),
        P("wide", "narrow"),
        P("wide"),
        P("narrow"),
    )
    return jax.shard_map(
        functools.partial(local, mesh.shape["wide"], mesh.shape["narrow"]),
        mesh=mesh, in_specs=placed, out_specs=P(None, "wide", "narrow"), check_vma=False,
    )
```

```python
import functools
import math

import jax
import jax.numpy as jnp
from jax import lax
from jax.experimental import pallas as pl
from jax.experimental.pallas import tpu as pltpu
from jax.sharding import PartitionSpec as P

MESH = pl.DeviceIdType.MESH
VM = pl.BlockSpec(memory_space=pltpu.VMEM)
CHUNKS = (4, 4)
PIECES = 4


def spread_kernel(dims, m, x_ref, psi_ref, phi_ref, xs_ref, psis_ref, phis_ref, xs_sem, xr_sem, fs_sem, fr_sem,
                  ps_sem, pr_sem, own_sem, gs_sem, gr_sem):
    zs, ys, xs = dims
    n = zs * ys * xs
    w = lax.axis_index("wide")
    c = lax.axis_index("narrow")
    spot = (w // (ys * xs), lax.rem(w // xs, ys), lax.rem(w, xs))
    columns = phi_ref.shape[1] // PIECES

    def moved(at, axis, by):
        at = list(at)
        at[axis] = lax.rem(at[axis] + by, dims[axis])
        return tuple(at)

    def flat(at):
        return (at[0] * ys + at[1]) * xs + at[2]

    def psi_copy(slot, peer, k):
        return pltpu.make_async_remote_copy(
            src_ref=psi_ref, dst_ref=psis_ref.at[slot], send_sem=ps_sem.at[k], recv_sem=pr_sem.at[slot],
            device_id=(w, peer), device_id_type=MESH)

    def x_copy(slot, peer, k):
        return pltpu.make_async_remote_copy(
            src_ref=x_ref, dst_ref=xs_ref.at[c, slot], send_sem=xs_sem.at[k], recv_sem=xr_sem.at[slot],
            device_id=(peer, c), device_id_type=MESH)

    def forward(src, slot_c, slot, peer, k):
        return pltpu.make_async_remote_copy(
            src_ref=src, dst_ref=xs_ref.at[slot_c, slot], send_sem=fs_sem.at[k, slot],
            recv_sem=fr_sem.at[slot_c, slot], device_id=(w, peer), device_id_type=MESH)

    def phi_copy(piece, block, peer, k, own=False):
        at = pl.ds(piece * columns, columns)
        held = phis_ref.at[block, :, at]
        return pltpu.make_async_remote_copy(
            src_ref=phi_ref.at[:, at] if own else held, dst_ref=held, send_sem=gs_sem.at[piece, k],
            recv_sem=gr_sem.at[piece, block], device_id=(peer, c), device_id_type=MESH)

    sent = [[] for _ in range(PIECES)]

    def phi_send(piece, block, axes, own=False):
        for axis in axes:
            for by in range(1, dims[axis]):
                copy = phi_copy(piece, block, flat(moved(spot, axis, by)), len(sent[piece]), own)
                copy.start()
                sent[piece].append(copy)

    def order(piece):
        return (0, 1, 2) if piece % 2 == 0 else (0, 2, 1)

    def arrivals(piece, stage):
        axes = order(piece)
        found = [spot]
        for axis in axes[:stage]:
            found = [moved(at, axis, by) for at in found for by in range(dims[axis])]
        axis = axes[stage]
        return [flat(moved(at, axis, dims[axis] - by)) for by in range(1, dims[axis]) for at in found]

    for piece in range(PIECES):
        phi_send(piece, w, order(piece), own=True)

    @pl.loop(1, n)
    def _(i):
        x_copy(w, lax.rem(w + i, n), i).start()

    @pl.loop(1, m)
    def _(j):
        forward(x_ref, c, w, lax.rem(c + j, m), j).start()
        psi_copy(c, lax.rem(c + j, m), j).start()

    own_x = pltpu.make_async_copy(x_ref, xs_ref.at[c, w], own_sem.at[0])
    own_psi = pltpu.make_async_copy(psi_ref, psis_ref.at[c], own_sem.at[1])
    own_phi = pltpu.make_async_copy(phi_ref, phis_ref.at[w], own_sem.at[2])
    own_x.start()
    own_psi.start()
    own_phi.start()

    for step in range(PIECES + 1):
        for stage in (1, 0):
            piece = step - stage
            if 0 <= piece < PIECES:
                for block in arrivals(piece, stage):
                    phi_copy(piece, block, w, 0).wait_recv()
                    phi_send(piece, block, order(piece)[stage + 1:])

    @pl.loop(1, n)
    def _(i):
        src = lax.rem(w + n - i, n)
        x_copy(src, w, i).wait_recv()

        @pl.loop(1, m)
        def _(j):
            forward(xs_ref.at[c, src], c, src, lax.rem(c + j, m), j).start()

    own_x.wait()
    own_psi.wait()
    own_phi.wait()

    @pl.loop(1, m)
    def _(j):
        other = lax.rem(c + m - j, m)
        psi_copy(other, c, j).wait_recv()
        psi_copy(c, c, j).wait_send()

        @pl.loop(0, n)
        def _(i):
            forward(x_ref, other, i, c, j).wait_recv()
            forward(x_ref, c, i, c, j).wait_send()

    @pl.loop(1, n)
    def _(i):
        x_copy(w, w, i).wait_send()

    for piece in range(PIECES):
        for block in arrivals(piece, 2):
            phi_copy(piece, block, w, 0).wait_recv()
        for copy in sent[piece]:
            copy.wait_send()


def spread(dims, m, x_trial, psi_orb, phi_piece):
    n = math.prod(dims)
    return pl.pallas_call(
        functools.partial(spread_kernel, dims, m),
        out_shape=(
            jax.ShapeDtypeStruct((m, n) + x_trial.shape, jnp.float32),
            jax.ShapeDtypeStruct((m,) + psi_orb.shape, jnp.float32),
            jax.ShapeDtypeStruct((n,) + phi_piece.shape, jnp.float32),
        ),
        in_specs=[VM, VM, VM],
        out_specs=(VM, VM, pl.BlockSpec(memory_space=pl.ANY)),
        scratch_shapes=[
            pltpu.SemaphoreType.DMA((n,)),
            pltpu.SemaphoreType.DMA((n,)),
            pltpu.SemaphoreType.DMA((m, n)),
            pltpu.SemaphoreType.DMA((m, n)),
            pltpu.SemaphoreType.DMA((m,)),
            pltpu.SemaphoreType.DMA((m,)),
            pltpu.SemaphoreType.DMA((3,)),
            pltpu.SemaphoreType.DMA((PIECES, n)),
            pltpu.SemaphoreType.DMA((PIECES, n)),
        ],
        compiler_params=pltpu.CompilerParams(has_side_effects=True),
        name="spread",
    )(x_trial, psi_orb, phi_piece)


def collect_kernel(n, part_ref, out_ref, got, s_sem, r_sem):
    w = lax.axis_index("wide")
    c = lax.axis_index("narrow")

    def copy(block, slot, peer, k):
        return pltpu.make_async_remote_copy(
            src_ref=part_ref.at[block], dst_ref=got.at[slot], send_sem=s_sem.at[k], recv_sem=r_sem.at[slot],
            device_id=(peer, c), device_id_type=MESH)

    @pl.loop(1, n)
    def _(i):
        peer = lax.rem(w + i, n)
        copy(peer, w, peer, i).start()

    out_ref[...] = part_ref[w]

    @pl.loop(1, n)
    def _(i):
        src = lax.rem(w + n - i, n)
        copy(src, src, w, i).wait_recv()
        out_ref[...] += got[src]

    @pl.loop(1, n)
    def _(i):
        copy(w, w, w, i).wait_send()


def collect(n, part):
    return pl.pallas_call(
        functools.partial(collect_kernel, n),
        out_shape=jax.ShapeDtypeStruct(part.shape[1:], jnp.float32),
        in_specs=[VM],
        out_specs=VM,
        scratch_shapes=[
            pltpu.VMEM(part.shape, jnp.float32),
            pltpu.SemaphoreType.DMA((n,)),
            pltpu.SemaphoreType.DMA((n,)),
        ],
        compiler_params=pltpu.CompilerParams(has_side_effects=True),
        name="collect",
    )(part)


def halves(a):
    high = a.astype(jnp.bfloat16)
    return high, (a - high.astype(jnp.float32)).astype(jnp.bfloat16)


def dot3(a, b, dims):
    def one(p, q):
        return lax.dot_general(p, q, (dims, ((), ())), preferred_element_type=jnp.float32)

    return one(a[0], b[0]) + (one(a[0], b[1]) + one(a[1], b[0]))


def tile_kernel(first, rows, half_ref, phi_ref, screened_ref, *refs):
    if first:
        back_ref, high, low = refs
    else:
        sum_ref, back_ref, high, low = refs
    trials, points, _ = half_ref.shape
    steps = points // rows

    @pl.when(pl.program_id(0) == 0)
    def _():
        for t in range(trials):
            @pl.loop(0, steps)
            def _(r):
                at = pl.ds(pl.multiple_of(r * rows, rows), rows)
                high[t, at], low[t, at] = halves(half_ref[t, at])
                back_ref[t, at] = jnp.zeros_like(half_ref[t, at]) if first else sum_ref[t, at]

    phi = halves(phi_ref[...])

    @pl.loop(0, steps)
    def _(r):
        at = pl.ds(pl.multiple_of(r * rows, rows), rows)
        for t in range(trials):
            pair = dot3((high[t, at], low[t, at]), phi, ((1,), (0,))) * screened_ref[at]
            back_ref[t, at] += dot3(halves(pair), phi, ((1,), (1,)))


def tile(half_map, phi, screened, start, back):
    trials, points, orbitals = half_map.shape
    width = phi.shape[1]
    columns = math.gcd(math.gcd(width, start) if start else width, 512)
    rows = math.gcd(points, 256)
    offset = start // columns
    whole = pl.BlockSpec((trials, points, orbitals), lambda s: (0, 0, 0))
    specs = [
        whole,
        pl.BlockSpec((orbitals, columns), lambda s: (0, s)),
        pl.BlockSpec((points, columns), lambda s: (0, s + offset)),
    ]
    args = [half_map, phi, screened]
    if back is not None:
        specs.append(whole)
        args.append(back)
    return pl.pallas_call(
        functools.partial(tile_kernel, back is None, rows),
        grid=(width // columns,),
        out_shape=jax.ShapeDtypeStruct(half_map.shape, jnp.float32),
        in_specs=specs,
        out_specs=whole,
        scratch_shapes=[pltpu.VMEM(half_map.shape, jnp.bfloat16)] * 2,
        input_output_aliases={3: 0} if back is not None else {},
        cost_estimate=pl.CostEstimate(
            flops=12 * trials * points * orbitals * width,
            bytes_accessed=4 * (points * width + orbitals * width + 3 * trials * points * orbitals),
            transcendentals=0,
        ),
        name="tile",
    )(*args)


def local(dims, m, x_trial, psi_orb, phi_orb, screened, eps_val, eps_cond):
    high = lax.Precision.HIGH
    n = math.prod(dims)
    orbitals, width = phi_orb.shape
    cut = width * CHUNKS[0] // sum(CHUNKS)
    late = lax.all_gather(lax.slice_in_dim(phi_orb, cut, width, axis=1), "wide", axis=0, tiled=True)
    x_all, psi_all, early = spread(dims, m, x_trial, psi_orb, lax.slice_in_dim(phi_orb, 0, cut, axis=1))
    phi_cols = ((0, early.reshape(n * orbitals, cut)), (cut, late))
    trials, vals, conds = x_trial.shape
    psi_rows = psi_all.reshape(m * psi_orb.shape[0], psi_orb.shape[1])
    x_whole = jnp.transpose(x_all, (2, 1, 3, 0, 4)).reshape(trials, n * vals, m * conds)
    back = None
    half_map = jnp.einsum("vr,tvc->trc", psi_rows, x_whole, precision=high)
    for start, phi in phi_cols:
        back = tile(half_map, phi, screened, start, back)
    summed = lax.psum_scatter(back, "narrow", scatter_dimension=2, tiled=True)
    part = jnp.einsum("vr,trc->vtc", psi_rows, summed, precision=high)
    part = jnp.swapaxes(part.reshape(n, vals, trials, conds), 1, 2)
    kernel = collect(n, part)
    energy_gap = eps_cond[None, None, :] - eps_val[None, :, None]
    return kernel + energy_gap * x_trial


def grid_of(mesh):
    n = mesh.shape["wide"]
    places = [getattr(d, "coords", None) for d in mesh.devices.reshape(n, -1)[:, 0]]
    if None in places:
        return 1, 1, n
    xs, ys = (len({p[axis] for p in places}) for axis in (0, 1))
    return (n // (xs * ys), ys, xs) if n % (xs * ys) == 0 else (1, 1, n)


def solution(mesh):
    placed = (
        P(None, "wide", "narrow"),
        P("narrow", "wide"),
        P("wide", "narrow"),
        P("wide", "narrow"),
        P("wide"),
        P("narrow"),
    )
    return jax.shard_map(
        functools.partial(local, grid_of(mesh), mesh.shape["narrow"]),
        mesh=mesh, in_specs=placed, out_specs=P(None, "wide", "narrow"), check_vma=False,
    )
```

```python
import functools
import math

import jax
import jax.numpy as jnp
from jax import lax
from jax.experimental import pallas as pl
from jax.experimental.pallas import tpu as pltpu
from jax.sharding import PartitionSpec as P

MESH = pl.DeviceIdType.MESH
VM = pl.BlockSpec(memory_space=pltpu.VMEM)
CHUNKS = (3, 5)
PIECES = 6
ROWS = 1024
COLUMNS = 512
UNROLL = 1


def spread_kernel(dims, m, x_ref, psi_ref, phi_ref, xs_ref, psis_ref, phis_ref, xs_sem, xr_sem, fs_sem, fr_sem,
                  ps_sem, pr_sem, own_sem, gs_sem, gr_sem):
    zs, ys, xs = dims
    n = zs * ys * xs
    w = lax.axis_index("wide")
    c = lax.axis_index("narrow")
    spot = (w // (ys * xs), lax.rem(w // xs, ys), lax.rem(w, xs))
    columns = phi_ref.shape[1] // PIECES

    def moved(at, axis, by):
        at = list(at)
        at[axis] = lax.rem(at[axis] + by, dims[axis])
        return tuple(at)

    def flat(at):
        return (at[0] * ys + at[1]) * xs + at[2]

    def psi_copy(slot, peer, k):
        return pltpu.make_async_remote_copy(
            src_ref=psi_ref, dst_ref=psis_ref.at[slot], send_sem=ps_sem.at[k], recv_sem=pr_sem.at[slot],
            device_id=(w, peer), device_id_type=MESH)

    def x_copy(slot, peer, k):
        return pltpu.make_async_remote_copy(
            src_ref=x_ref, dst_ref=xs_ref.at[c, slot], send_sem=xs_sem.at[k], recv_sem=xr_sem.at[slot],
            device_id=(peer, c), device_id_type=MESH)

    def forward(src, slot_c, slot, peer, k):
        return pltpu.make_async_remote_copy(
            src_ref=src, dst_ref=xs_ref.at[slot_c, slot], send_sem=fs_sem.at[k, slot],
            recv_sem=fr_sem.at[slot_c, slot], device_id=(w, peer), device_id_type=MESH)

    def phi_copy(piece, block, peer, k, own=False):
        at = pl.ds(piece * columns, columns)
        held = phis_ref.at[block, :, at]
        return pltpu.make_async_remote_copy(
            src_ref=phi_ref.at[:, at] if own else held, dst_ref=held, send_sem=gs_sem.at[piece, k],
            recv_sem=gr_sem.at[piece, block], device_id=(peer, c), device_id_type=MESH)

    sent = [[] for _ in range(PIECES)]

    def phi_send(piece, block, axes, own=False):
        for axis in axes:
            for by in range(1, dims[axis]):
                copy = phi_copy(piece, block, flat(moved(spot, axis, by)), len(sent[piece]), own)
                copy.start()
                sent[piece].append(copy)

    def order(piece):
        return (0, 1, 2) if piece % 2 == 0 else (0, 2, 1)

    def arrivals(piece, stage):
        axes = order(piece)
        found = [spot]
        for axis in axes[:stage]:
            found = [moved(at, axis, by) for at in found for by in range(dims[axis])]
        axis = axes[stage]
        return [flat(moved(at, axis, dims[axis] - by)) for by in range(1, dims[axis]) for at in found]

    for piece in range(PIECES):
        phi_send(piece, w, order(piece), own=True)

    @pl.loop(1, n)
    def _(i):
        x_copy(w, lax.rem(w + i, n), i).start()

    @pl.loop(1, m)
    def _(j):
        forward(x_ref, c, w, lax.rem(c + j, m), j).start()
        psi_copy(c, lax.rem(c + j, m), j).start()

    own_x = pltpu.make_async_copy(x_ref, xs_ref.at[c, w], own_sem.at[0])
    own_psi = pltpu.make_async_copy(psi_ref, psis_ref.at[c], own_sem.at[1])
    own_phi = pltpu.make_async_copy(phi_ref, phis_ref.at[w], own_sem.at[2])
    own_x.start()
    own_psi.start()
    own_phi.start()

    for step in range(PIECES + 1):
        for stage in (1, 0):
            piece = step - stage
            if 0 <= piece < PIECES:
                for block in arrivals(piece, stage):
                    phi_copy(piece, block, w, 0).wait_recv()
                    phi_send(piece, block, order(piece)[stage + 1:])

    @pl.loop(1, n)
    def _(i):
        src = lax.rem(w + n - i, n)
        x_copy(src, w, i).wait_recv()

        @pl.loop(1, m)
        def _(j):
            forward(xs_ref.at[c, src], c, src, lax.rem(c + j, m), j).start()

    own_x.wait()
    own_psi.wait()
    own_phi.wait()

    @pl.loop(1, m)
    def _(j):
        other = lax.rem(c + m - j, m)
        psi_copy(other, c, j).wait_recv()
        psi_copy(c, c, j).wait_send()

        @pl.loop(0, n)
        def _(i):
            forward(x_ref, other, i, c, j).wait_recv()
            forward(x_ref, c, i, c, j).wait_send()

    @pl.loop(1, n)
    def _(i):
        x_copy(w, w, i).wait_send()

    for piece in range(PIECES):
        for block in arrivals(piece, 2):
            phi_copy(piece, block, w, 0).wait_recv()
        for copy in sent[piece]:
            copy.wait_send()


def spread(dims, m, x_trial, psi_orb, phi_piece):
    n = math.prod(dims)
    return pl.pallas_call(
        functools.partial(spread_kernel, dims, m),
        out_shape=(
            jax.ShapeDtypeStruct((m, n) + x_trial.shape, jnp.float32),
            jax.ShapeDtypeStruct((m,) + psi_orb.shape, jnp.float32),
            jax.ShapeDtypeStruct((n,) + phi_piece.shape, jnp.float32),
        ),
        in_specs=[VM, VM, VM],
        out_specs=(VM, VM, pl.BlockSpec(memory_space=pl.ANY)),
        scratch_shapes=[
            pltpu.SemaphoreType.DMA((n,)),
            pltpu.SemaphoreType.DMA((n,)),
            pltpu.SemaphoreType.DMA((m, n)),
            pltpu.SemaphoreType.DMA((m, n)),
            pltpu.SemaphoreType.DMA((m,)),
            pltpu.SemaphoreType.DMA((m,)),
            pltpu.SemaphoreType.DMA((3,)),
            pltpu.SemaphoreType.DMA((PIECES, n)),
            pltpu.SemaphoreType.DMA((PIECES, n)),
        ],
        compiler_params=pltpu.CompilerParams(has_side_effects=True),
        name="spread",
    )(x_trial, psi_orb, phi_piece)


def collect_kernel(n, part_ref, out_ref, got, s_sem, r_sem):
    w = lax.axis_index("wide")
    c = lax.axis_index("narrow")

    def copy(block, slot, peer, k):
        return pltpu.make_async_remote_copy(
            src_ref=part_ref.at[block], dst_ref=got.at[slot], send_sem=s_sem.at[k], recv_sem=r_sem.at[slot],
            device_id=(peer, c), device_id_type=MESH)

    @pl.loop(1, n)
    def _(i):
        peer = lax.rem(w + i, n)
        copy(peer, w, peer, i).start()

    out_ref[...] = part_ref[w]

    @pl.loop(1, n)
    def _(i):
        src = lax.rem(w + n - i, n)
        copy(src, src, w, i).wait_recv()
        out_ref[...] += got[src]

    @pl.loop(1, n)
    def _(i):
        copy(w, w, w, i).wait_send()


def collect(n, part):
    return pl.pallas_call(
        functools.partial(collect_kernel, n),
        out_shape=jax.ShapeDtypeStruct(part.shape[1:], jnp.float32),
        in_specs=[VM],
        out_specs=VM,
        scratch_shapes=[
            pltpu.VMEM(part.shape, jnp.float32),
            pltpu.SemaphoreType.DMA((n,)),
            pltpu.SemaphoreType.DMA((n,)),
        ],
        compiler_params=pltpu.CompilerParams(has_side_effects=True),
        name="collect",
    )(part)


def halves(a):
    high = a.astype(jnp.bfloat16)
    return high, (a - high.astype(jnp.float32)).astype(jnp.bfloat16)


def dot3(a, b, dims):
    def one(p, q):
        return lax.dot_general(p, q, (dims, ((), ())), preferred_element_type=jnp.float32)

    return one(a[0], b[0]) + (one(a[0], b[1]) + one(a[1], b[0]))


def tile_kernel(first, rows, half_ref, phi_ref, screened_ref, *refs):
    if first:
        back_ref, high, low = refs
    else:
        sum_ref, back_ref, high, low = refs
    trials, points, _ = half_ref.shape
    steps = points // rows

    @pl.when(pl.program_id(0) == 0)
    def _():
        for t in range(trials):
            @pl.loop(0, steps)
            def _(r):
                at = pl.ds(pl.multiple_of(r * rows, rows), rows)
                high[t, at], low[t, at] = halves(half_ref[t, at])
                back_ref[t, at] = jnp.zeros_like(half_ref[t, at]) if first else sum_ref[t, at]

    phi = halves(phi_ref[...])

    @pl.loop(0, steps, unroll=UNROLL)
    def _(r):
        at = pl.ds(pl.multiple_of(r * rows, rows), rows)
        for t in range(trials):
            pair = dot3((high[t, at], low[t, at]), phi, ((1,), (0,))) * screened_ref[at]
            back_ref[t, at] += dot3(halves(pair), phi, ((1,), (1,)))


def tile(half_map, phi, screened, start, back):
    trials, points, orbitals = half_map.shape
    width = phi.shape[1]
    columns = math.gcd(math.gcd(width, start) if start else width, COLUMNS)
    rows = math.gcd(points, ROWS)
    offset = start // columns
    whole = pl.BlockSpec((trials, points, orbitals), lambda s: (0, 0, 0))
    specs = [
        whole,
        pl.BlockSpec((orbitals, columns), lambda s: (0, s)),
        pl.BlockSpec((points, columns), lambda s: (0, s + offset)),
    ]
    args = [half_map, phi, screened]
    if back is not None:
        specs.append(whole)
        args.append(back)
    return pl.pallas_call(
        functools.partial(tile_kernel, back is None, rows),
        grid=(width // columns,),
        out_shape=jax.ShapeDtypeStruct(half_map.shape, jnp.float32),
        in_specs=specs,
        out_specs=whole,
        scratch_shapes=[pltpu.VMEM(half_map.shape, jnp.bfloat16)] * 2,
        input_output_aliases={3: 0} if back is not None else {},
        cost_estimate=pl.CostEstimate(
            flops=12 * trials * points * orbitals * width,
            bytes_accessed=4 * (points * width + orbitals * width + 3 * trials * points * orbitals),
            transcendentals=0,
        ),
        name="tile",
    )(*args)


def local(dims, m, x_trial, psi_orb, phi_orb, screened, eps_val, eps_cond):
    high = lax.Precision.HIGH
    n = math.prod(dims)
    orbitals, width = phi_orb.shape
    cut = width * CHUNKS[0] // sum(CHUNKS)
    late = lax.all_gather(lax.slice_in_dim(phi_orb, cut, width, axis=1), "wide", axis=0, tiled=True)
    x_all, psi_all, early = spread(dims, m, x_trial, psi_orb, lax.slice_in_dim(phi_orb, 0, cut, axis=1))
    phi_cols = ((0, early.reshape(n * orbitals, cut)), (cut, late))
    trials, vals, conds = x_trial.shape
    psi_rows = psi_all.reshape(m * psi_orb.shape[0], psi_orb.shape[1])
    x_whole = jnp.transpose(x_all, (2, 1, 3, 0, 4)).reshape(trials, n * vals, m * conds)
    back = None
    half_map = jnp.einsum("vr,tvc->trc", psi_rows, x_whole, precision=high)
    for start, phi in phi_cols:
        back = tile(half_map, phi, screened, start, back)
    summed = lax.psum_scatter(back, "narrow", scatter_dimension=2, tiled=True)
    part = jnp.einsum("vr,trc->vtc", psi_rows, summed, precision=high)
    part = jnp.swapaxes(part.reshape(n, vals, trials, conds), 1, 2)
    kernel = collect(n, part)
    energy_gap = eps_cond[None, None, :] - eps_val[None, :, None]
    return kernel + energy_gap * x_trial


def grid_of(mesh):
    n = mesh.shape["wide"]
    places = [getattr(d, "coords", None) for d in mesh.devices.reshape(n, -1)[:, 0]]
    if None in places:
        return 1, 1, n
    xs, ys = (len({p[axis] for p in places}) for axis in (0, 1))
    return (n // (xs * ys), ys, xs) if n % (xs * ys) == 0 else (1, 1, n)


def solution(mesh):
    placed = (
        P(None, "wide", "narrow"),
        P("narrow", "wide"),
        P("wide", "narrow"),
        P("wide", "narrow"),
        P("wide"),
        P("narrow"),
    )
    return jax.shard_map(
        functools.partial(local, grid_of(mesh), mesh.shape["narrow"]),
        mesh=mesh, in_specs=placed, out_specs=P(None, "wide", "narrow"), check_vma=False,
    )
```
